128 devices in a mesh: wide: 16 (over x_hi, z, core), narrow: 8 (over y, x_lo).
Axes of the slice: x: 4 (x_hi: 2, x_lo: 2; x = x_hi * 2 + x_lo), y: 4, z: 4, core: 2. Of those that a mesh axis runs over, the one named last changes fastest.
Arguments:
- replica_grads: bfloat16 [128, 16, 512, 512], P(('wide', 'narrow')), may hold values from -0.0625 to 0.0625
- owner_table: int32 [16], replicated, may hold values from 0 to 15, as said below
- left_stat: float32 [16, 512, 512], P('wide'), may hold values from -1 to 5, as said below
- right_stat: float32 [16, 512, 512], P('wide'), may hold values from -1 to 5, as said below
- left_root: float32 [16, 512, 512], P('wide'), may hold values from -1 to 2, as said below
- right_root: float32 [16, 512, 512], P('wide'), may hold values from -1 to 2, as said below
Outputs:
- directions: float32 [16, 512, 512], P(None, 'narrow')
- left_new: float32 [16, 512, 512], P('wide')
- right_new: float32 [16, 512, 512], P('wide')
- left_inverse: float32 [16, 512, 512], P('wide')
- right_inverse: float32 [16, 512, 512], P('wide')
The draws below stay inside these ranges and needn't reach their ends.
Inputs may be any that keep to these rules, and one draw needn't show every extreme that they name: `owner_table`: the 16 entries are distinct, so every slot is named once. `left_stat`: each slot's matrix is symmetric positive definite. `right_stat`: each slot's matrix is symmetric positive definite. `left_root`: each slot's matrix is symmetric. `right_root`: each slot's matrix is symmetric.
All inputs are finite; a program needn't handle non-finite values.
Results may differ from the reference program's by a relative error of at most 0.0003.
Values sent between devices are 32-bit elements; how exact they have to be, the bound alone decides.
No kernel may reach another device: no remote copies, remote signals or barrier semaphores. Data moves between devices by JAX's collectives and lax.ppermute only.
A program may use at most 128 MiB of HBM per device.

```python
import jax
import jax.numpy as jnp
from jax import lax

BLOCK = 512
BLOCKS = 16
REPLICAS = 128
N_WIDE = 16


def symmetric_field(key, lowest, highest, spread):
    first_key, second_key = jax.random.split(key)
    noise = jax.random.normal(first_key, (N_WIDE, BLOCK, BLOCK), jnp.float32)
    noise = jnp.clip(noise, -5.0, 5.0)
    noise = (noise + jnp.swapaxes(noise, 1, 2)) * (spread / (2.0 * BLOCK) ** 0.5)
    diagonal = jax.random.uniform(second_key, (N_WIDE, BLOCK), jnp.float32, lowest, highest)
    return noise + diagonal[:, :, None] * jnp.eye(BLOCK, dtype=jnp.float32)


def draw_owner_table(key, part):
    return jax.random.permutation(key, N_WIDE)[:BLOCKS].astype(jnp.int32)


def draw_left_stat(key, part):
    return symmetric_field(jax.random.fold_in(key, 11), 1.0, 2.0, 0.3)


def draw_right_stat(key, part):
    return symmetric_field(jax.random.fold_in(key, 12), 1.0, 2.0, 0.3)


def draw_left_root(key, part):
    return symmetric_field(jax.random.fold_in(key, 13), 0.6, 0.9, 0.1)


def draw_right_root(key, part):
    return symmetric_field(jax.random.fold_in(key, 14), 0.6, 0.9, 0.1)


def steps_of(rng, extent, cuts, low, top_value):
    gain = 1.0
    for axis_at, shards_of in cuts:
        heights = jax.random.uniform(jax.random.fold_in(jax.random.fold_in(rng, 6), axis_at), (shards_of,), jnp.float32, low / len(cuts), top_value / len(cuts))
        gain = gain * jnp.repeat(jnp.exp(heights), extent[axis_at] // shards_of).reshape((-1,) + (1,) * (len(extent) - 1 - axis_at))
    return gain


def gaussian(stream_key, extent, scale, bound, cuts=(), kind=jnp.bfloat16):
    entries = scale * jax.random.normal(stream_key, extent, jnp.float32)
    if cuts:
        entries = entries * steps_of(stream_key, extent, cuts, -0.22, 0.18)
    return jnp.clip(entries, -bound, bound).astype(kind)


def setup_inputs(seed: int = 0) -> dict:
    keys = jax.random.split(jax.random.key(seed), 7)
    return {
        "replica_grads": gaussian(keys[0], (REPLICAS, BLOCKS, BLOCK, BLOCK), (REPLICAS * BLOCK // 8) ** -0.5, 0.0625, ((0, 128),)),
        "owner_table": draw_owner_table(jax.random.fold_in(keys[6], 71), 0),
        "left_stat": draw_left_stat(jax.random.fold_in(keys[6], 71), 0),
        "right_stat": draw_right_stat(jax.random.fold_in(keys[6], 71), 0),
        "left_root": draw_left_root(jax.random.fold_in(keys[6], 71), 0),
        "right_root": draw_right_root(jax.random.fold_in(keys[6], 71), 0),
    }


decay_rate = 0.95


def matmul_high(first, second):
    return jnp.dot(first, second, precision=lax.Precision.HIGHEST, preferred_element_type=jnp.float32)


def gram_right(matrix):
    return lax.dot_general(matrix, matrix, (((0,), (0,)), ((), ())), precision=lax.Precision.HIGHEST, preferred_element_type=jnp.float32)


def newton_step(old_root, statistic):
    squared = matmul_high(old_root, old_root)
    fourth_power = matmul_high(squared, squared)
    coupled = matmul_high(fourth_power, statistic)
    return (5.0 * old_root - matmul_high(old_root, coupled)) / 4.0


def update_slot(items):
    slot_grad, left_old, right_old, left_prev, right_prev = items
    left_value = decay_rate * left_old + (1.0 - decay_rate) * matmul_high(slot_grad, slot_grad.T)
    right_value = decay_rate * right_old + (1.0 - decay_rate) * gram_right(slot_grad)
    left_next = newton_step(left_prev, left_value)
    right_next = newton_step(right_prev, right_value)
    preconditioned = matmul_high(matmul_high(left_next, slot_grad), right_next)
    return left_value, right_value, left_next, right_next, preconditioned


def reference(replica_grads, owner_table, left_stat, right_stat, left_root, right_root):
    summed = jnp.sum(replica_grads, axis=0, dtype=jnp.float32)
    slot_grads = jnp.zeros((N_WIDE, BLOCK, BLOCK), jnp.float32).at[owner_table].set(summed)
    results = lax.map(update_slot, (slot_grads, left_stat, right_stat, left_root, right_root))
    directions = jnp.take(results[4], owner_table, axis=0)
    return directions, results[0], results[1], results[2], results[3]
```

```python
import functools

import jax
import jax.numpy as jnp
from jax import lax
from jax.experimental import pallas as pl
from jax.experimental.pallas import tpu as pltpu
from jax.sharding import Mesh, PartitionSpec as P

AXES = ("xh", "z", "core", "y", "xl")
SIZES = (2, 4, 2, 4, 2)
DECAY = 0.95
ORDER = 512
ROWS = 64
VMEM_LIMIT = 48 * 1024 * 1024
STREAM_PAIRS = (tuple(range(0, 6)), tuple(range(6, 11)), tuple(range(11, 16)))


def index_of(x, y, z, c):
    return ((((x >> 1) * 4 + z) * 2 + c) * 4 + y) * 2 + (x & 1)


def permutation(move):
    return [
        (index_of(x, y, z, c), index_of(*move(x, y, z, c)))
        for x in range(4)
        for y in range(4)
        for z in range(4)
        for c in range(2)
    ]


def axis_move(axis, masks):
    def move(x, y, z, c):
        place = [x, y, z]
        place[axis] ^= masks[c]
        return (*place, c)

    return permutation(move)


CORE_SWAP = permutation(lambda x, y, z, c: (x, y, z, 1 - c))


def send(value, pairs):
    return lax.ppermute(value, AXES, pairs)


def place():
    xl = lax.axis_index("xl")
    x = lax.axis_index("xh") * 2 + xl
    return x, lax.axis_index("y"), lax.axis_index("z"), lax.axis_index("core")


def split(value):
    high = value.astype(jnp.bfloat16)
    low = (value - high.astype(jnp.float32)).astype(jnp.bfloat16)
    return high, low


def product(first, second, dims=((1,), (0,))):
    fh, fl = first
    sh, sl = second

    def dot(a, b):
        return lax.dot_general(a, b, (dims, ((), ())), preferred_element_type=jnp.float32)

    return dot(fh, sh) + (dot(fh, sl) + dot(fl, sh))


NT = ((1,), (1,))
TN = ((0,), (0,))


def fill_inverse(owner_ref, inverse_ref):
    for b in range(16):
        inverse_ref[owner_ref[b]] = b


def pack_kernel(own, parts, scalars_ref, owner_ref, grads_ref, *rest):
    outs = rest[: len(parts)]
    blocks, inverse, sems = rest[len(parts) :]
    x, y, z, c = (scalars_ref[i] for i in range(4))
    target = c if own else 1 - c
    fill_inverse(owner_ref, inverse)

    def fetch(g):
        return pltpu.make_async_copy(
            grads_ref.at[0, inverse[g * 2 + target]], blocks.at[g], sems.at[g]
        )

    for g in range(8):
        fetch(g).start()
    for g in range(8):
        fetch(g).wait()
    p1 = 1 + 2 * target
    p2 = 3 - 2 * target
    for (stream, half), out in zip(parts, outs):

        def body(k, carry, stream=stream, half=half, out=out):
            bits = [(k >> s) & 1 for s in (4, 3, 2, 1, 0)]
            steps = [
                (half * p1) ^ (bits[0] * p2),
                (bits[1] * p1) ^ (bits[2] * p2),
                (bits[3] * p1) ^ (bits[4] * p2),
            ]
            moved = [x, y, z]
            for i in range(3):
                moved[(stream + i) % 3] = moved[(stream + i) % 3] ^ steps[i]
            xd, yd, zd = moved
            g = (xd >> 1) * 4 + zd
            row = (yd * 2 + (xd & 1)) * ROWS
            for i, pair in enumerate(STREAM_PAIRS[stream]):
                start = pl.multiple_of(row + (pair // 4) * 16, 16)
                col = (pair % 4) * 128
                value = blocks[g, pl.ds(start, 16), col : col + 128]
                out[k, 2 * i : 2 * i + 2] = value.astype(jnp.float32).reshape(2, 8, 128)
            return carry

        lax.fori_loop(0, 32, body, 0, unroll=2)


def pack(own, parts, scalars, owner_table, grads):
    smem = pl.BlockSpec(memory_space=pltpu.SMEM)
    vmem = pl.BlockSpec(memory_space=pltpu.VMEM)
    return pl.pallas_call(
        functools.partial(pack_kernel, own, parts),
        out_shape=[
            jax.ShapeDtypeStruct((32, 2 * len(STREAM_PAIRS[s]), 8, 128), jnp.float32)
            for s, _ in parts
        ],
        in_specs=[smem, smem, pl.BlockSpec(memory_space=pl.ANY)],
        out_specs=[vmem] * len(parts),
        scratch_shapes=[
            pltpu.VMEM((8, ORDER, ORDER), jnp.bfloat16),
            pltpu.SMEM((16,), jnp.int32),
            pltpu.SemaphoreType.DMA((8,)),
        ],
        compiler_params=pltpu.CompilerParams(vmem_limit_bytes=VMEM_LIMIT),
        name="pack_own" if own else "pack_other",
    )(scalars, owner_table, grads)


def roots_kernel(ls_ref, rs_ref, lr_ref, rr_ref, lc_ref, lk_ref, rc_ref, rk_ref):
    for stat_ref, root_ref, c_ref, k_ref in (
        (ls_ref, lr_ref, lc_ref, lk_ref),
        (rs_ref, rr_ref, rc_ref, rk_ref),
    ):
        root = root_ref[0]
        parts = split(root)
        square = split(product(parts, parts))
        fourth = split(product(square, square))
        fifth = product(parts, fourth)
        k_ref[...] = fifth * ((1.0 - DECAY) / 4.0)
        c_ref[...] = 1.25 * root - (DECAY / 4.0) * product(split(fifth), split(stat_ref[0]))


def whole(count):
    return [pl.BlockSpec(memory_space=pltpu.VMEM)] * count


def roots(left_stat, right_stat, left_root, right_root):
    return pl.pallas_call(
        roots_kernel,
        out_shape=[jax.ShapeDtypeStruct((ORDER, ORDER), jnp.float32)] * 4,
        in_specs=whole(4),
        out_specs=whole(4),
        compiler_params=pltpu.CompilerParams(vmem_limit_bytes=VMEM_LIMIT),
        name="roots",
    )(left_stat, right_stat, left_root, right_root)


def join_kernel(k0, r0, k1, r1, k2, r2, out):
    at = 0
    for kept, got in ((k0, r0), (k1, r1), (k2, r2)):
        count = kept.shape[1]
        out[at : at + count] = kept[0] + got[0]
        at += count


def join(pieces):
    return pl.pallas_call(
        join_kernel,
        out_shape=jax.ShapeDtypeStruct((32, 8, 128), jnp.float32),
        in_specs=whole(6),
        out_specs=pl.BlockSpec(memory_space=pltpu.VMEM),
        name="join",
    )(*pieces)


def assemble(narrow, pieces, grad):
    for m, piece in enumerate(pieces):
        row = (narrow ^ m) * ROWS
        for pair in range(16):
            col = (pair % 4) * 128
            start = pl.multiple_of(row + (pair // 4) * 16, 16)
            grad[pl.ds(start, 16), col : col + 128] = piece[2 * pair : 2 * pair + 2].reshape(16, 128)


def rows_kernel(scalars_ref, *refs):
    pieces = refs[:8]
    lc_ref, lk_ref, rc_ref, rk_ref, out, grad = refs[8:]
    narrow = scalars_ref[4]
    assemble(narrow, pieces, grad)
    g = split(grad[...])
    start = pl.multiple_of(narrow * ROWS, ROWS)
    inner = product(split(lk_ref[pl.ds(start, ROWS), :]), g)
    left = lc_ref[pl.ds(start, ROWS), :] - product(split(inner), g, NT)
    turned = split(product(split(left), g))
    inner = product(turned, split(rk_ref[...]))
    inner = product(split(inner), g, NT)
    out[...] = product(turned, split(rc_ref[...])) - product(split(inner), g)


def precondition_rows(scalars, pieces, constants):
    return pl.pallas_call(
        rows_kernel,
        out_shape=jax.ShapeDtypeStruct((ROWS, ORDER), jnp.float32),
        in_specs=[pl.BlockSpec(memory_space=pltpu.SMEM)] + whole(12),
        out_specs=pl.BlockSpec(memory_space=pltpu.VMEM),
        scratch_shapes=[pltpu.VMEM((ORDER, ORDER), jnp.float32)],
        compiler_params=pltpu.CompilerParams(vmem_limit_bytes=VMEM_LIMIT),
        name="rows",
    )(scalars, *pieces, *constants)


def stats_kernel(scalars_ref, *refs):
    pieces = refs[:8]
    lc_ref, lk_ref, rc_ref, rk_ref, ls_ref, rs_ref = refs[8:14]
    ln_ref, rn_ref, li_ref, ri_ref, grad = refs[14:]
    assemble(scalars_ref[4], pieces, grad)
    g = split(grad[...])
    for dims, stat_ref, c_ref, k_ref, new_ref, inv_ref in (
        (NT, ls_ref, lc_ref, lk_ref, ln_ref, li_ref),
        (TN, rs_ref, rc_ref, rk_ref, rn_ref, ri_ref),
    ):
        gram = product(g, g, dims)
        new_ref[0] = DECAY * stat_ref[0] + (1.0 - DECAY) * gram
        inv_ref[0] = c_ref[...] - product(split(k_ref[...]), split(gram))


def statistics(scalars, pieces, constants, left_stat, right_stat):
    return pl.pallas_call(
        stats_kernel,
        out_shape=[jax.ShapeDtypeStruct((1, ORDER, ORDER), jnp.float32)] * 4,
        in_specs=[pl.BlockSpec(memory_space=pltpu.SMEM)] + whole(14),
        out_specs=whole(4),
        scratch_shapes=[pltpu.VMEM((ORDER, ORDER), jnp.float32)],
        compiler_params=pltpu.CompilerParams(vmem_limit_bytes=VMEM_LIMIT),
        name="stats",
    )(scalars, *pieces, *constants, left_stat, right_stat)


def spread_kernel(scalars_ref, owner_ref, pair_ref, p0, p1, p2, p3, q0, q1, q2, q3, out, inverse, sems):
    x, z, c = scalars_ref[0], scalars_ref[2], scalars_ref[3]
    xh = x >> 1
    fill_inverse(owner_ref, inverse)
    copies = []

    def put(src, xd, zd, cd):
        slot = (xd * 4 + zd) * 2 + cd
        copies.append(pltpu.make_async_copy(src, out.at[inverse[slot]], sems.at[len(copies)]))

    for i in range(2):
        put(pair_ref.at[i], xh, z, c ^ i)
    put(p0, xh ^ 1, z, c)
    put(q0, xh ^ 1, z, 1 - c)
    for holder, group in ((c, (p1, p2, p3)), (1 - c, (q1, q2, q3))):
        for j, ref in enumerate(group):
            for i in range(2):
                put(ref.at[i], xh ^ holder, z ^ (j + 1), holder ^ i)
    for copy in copies:
        copy.start()
    for copy in copies:
        copy.wait()


def spread(scalars, owner_table, pieces):
    smem = pl.BlockSpec(memory_space=pltpu.SMEM)
    anywhere = pl.BlockSpec(memory_space=pl.ANY)
    return pl.pallas_call(
        spread_kernel,
        out_shape=jax.ShapeDtypeStruct((16, ROWS, ORDER), jnp.float32),
        in_specs=[smem, smem] + [anywhere] * 9,
        out_specs=anywhere,
        scratch_shapes=[pltpu.SMEM((16,), jnp.int32), pltpu.SemaphoreType.DMA((16,))],
        name="spread",
    )(scalars, owner_table, *pieces)


def local(replica_grads, owner_table, left_stat, right_stat, left_root, right_root):
    x, y, z, c = place()
    scalars = jnp.stack([x, y, z, c, y * 2 + (x & 1)]).astype(jnp.int32)
    streams = range(3)
    sends = [(s, 1) for s in streams]
    keeps = [(s, 0) for s in streams]
    other_send = pack(False, sends, scalars, owner_table, replica_grads)
    got_send = [send(other_send[s], CORE_SWAP) for s in streams]
    own_send = pack(True, sends, scalars, owner_table, replica_grads)
    other_keep = pack(False, keeps, scalars, owner_table, replica_grads)
    got_keep = [send(other_keep[s], CORE_SWAP) for s in streams]
    own_keep = pack(True, keeps, scalars, owner_table, replica_grads)
    outgoing = [own_send[s] + got_send[s] for s in streams]
    kept = [own_keep[s] + got_keep[s] for s in streams]
    constants = roots(left_stat, right_stat, left_root, right_root)
    tails = [None] * 3
    for step in range(6):
        masks = (1, 3) if step % 2 == 0 else (3, 1)
        for s in streams:
            got = send(outgoing[s], axis_move((s + step // 2) % 3, masks))
            if step == 5:
                tails[s] = (kept[s], got)
                continue
            half = kept[s].shape[0] // 2
            outgoing[s] = kept[s][half:] + got[half:]
            kept[s] = kept[s][:half] + got[:half]
    own = join([value for pair in tails for value in pair])
    pieces = [own] + [None] * 7
    for m in (1, 5, 3, 7, 4, 2, 6):
        pieces[m] = send(
            own, permutation(lambda x, y, z, c, m=m: (x ^ (m & 1), y ^ (m >> 1), z, c))
        )
    rows = precondition_rows(scalars, pieces, constants)
    both = jnp.stack([rows, send(rows, CORE_SWAP)])
    got = [None] * 4
    for j in (2, 1, 3):
        got[j] = send(both, permutation(lambda x, y, z, c, j=j: (x ^ (2 * c), y, z ^ j, c)))
    got[0] = send(rows, axis_move(0, (2, 2)))
    swapped = [send(value, CORE_SWAP) for value in got]
    left_new, right_new, left_inverse, right_inverse = statistics(
        scalars, pieces, constants, left_stat, right_stat
    )
    directions = spread(scalars, owner_table, [both] + got + swapped)
    return directions, left_new, right_new, left_inverse, right_inverse


def solution(mesh):
    fine = Mesh(mesh.devices.reshape(SIZES), AXES)
    wide = ("xh", "z", "core")
    narrow = ("y", "xl")
    slot = P(wide, None, None)
    return jax.shard_map(
        local,
        mesh=fine,
        in_specs=(P(wide + narrow, None, None, None), P(), slot, slot, slot, slot),
        out_specs=(P(None, narrow, None), slot, slot, slot, slot),
        check_vma=False,
    )
```

```python
import functools

import jax
import jax.numpy as jnp
from jax import lax
from jax.experimental import pallas as pl
from jax.experimental.pallas import tpu as pltpu
from jax.sharding import Mesh, PartitionSpec as P

AXES = ("xh", "z", "core", "y", "xl")
SIZES = (2, 4, 2, 4, 2)
DECAY = 0.95
ORDER = 512
ROWS = 64
VMEM_LIMIT = 20 * 1024 * 1024
SMALL_LIMIT = 8 * 1024 * 1024
STREAM_TILES = (range(0, 11), range(11, 22), range(22, 32))


def index_of(x, y, z, c):
    return ((((x >> 1) * 4 + z) * 2 + c) * 4 + y) * 2 + (x & 1)


def permutation(move):
    return [
        (index_of(x, y, z, c), index_of(*move(x, y, z, c)))
        for x in range(4)
        for y in range(4)
        for z in range(4)
        for c in range(2)
    ]


def axis_move(axis, masks):
    def move(x, y, z, c):
        place = [x, y, z]
        place[axis] ^= masks[c]
        return (*place, c)

    return permutation(move)


CORE_SWAP = permutation(lambda x, y, z, c: (x, y, z, 1 - c))


FLIP = (0, 0, 1)


def member(axis, core, coset, bit):
    variant = core ^ FLIP[axis]
    return (1 - variant) * ((bit << 1) | (bit ^ coset)) + variant * ((coset << 1) | bit)


def coset_of(axis, core, position):
    variant = core ^ FLIP[axis]
    return (1 - variant) * ((position ^ (position >> 1)) & 1) + variant * (position >> 1)


def first_masks(axis):
    return tuple(1 + 2 * (core ^ FLIP[axis]) for core in range(2))


BITS = (0, 1)
CUBES = [
    [
        index_of(member(0, c, qx, vx), member(1, c, qy, vy), member(2, c, qz, vz), c)
        for vx in BITS
        for vy in BITS
        for vz in BITS
    ]
    for c in BITS
    for qx in BITS
    for qy in BITS
    for qz in BITS
]


def send(value, pairs):
    return lax.ppermute(value, AXES, pairs)


def place():
    xl = lax.axis_index("xl")
    x = lax.axis_index("xh") * 2 + xl
    return x, lax.axis_index("y"), lax.axis_index("z"), lax.axis_index("core")


def split(value):
    high = value.astype(jnp.bfloat16)
    low = (value - high.astype(jnp.float32)).astype(jnp.bfloat16)
    return high, low


def product(first, second, dims=((1,), (0,))):
    fh, fl = first
    sh, sl = second

    def dot(a, b):
        return lax.dot_general(a, b, (dims, ((), ())), preferred_element_type=jnp.float32)

    return dot(fh, sh) + (dot(fh, sl) + dot(fl, sh))


NT = ((1,), (1,))
TN = ((0,), (0,))


def pack_kernel(parts, table_ref, blocks, *rest):
    extra, outs = rest[: -len(parts)], rest[-len(parts) :]
    if extra:
        roots_kernel(*extra)
    here = [table_ref[16 + i] for i in range(3)]
    c = table_ref[19]
    targets = [c if own else 1 - c for own, _, _ in parts]
    cosets = [[coset_of(i, target, here[i]) for i in range(3)] for target in targets]

    def body(k, carry):
        for (_, half, streams), target, coset, out in zip(parts, targets, cosets, outs):
            offset = STREAM_TILES[streams[0]][0]
            for stream in streams:
                flips = [0, 0, 0]
                flips[stream] = half
                flips[(stream + 1) % 3] = (k >> 4) & 1
                flips[(stream + 2) % 3] = (k >> 3) & 1
                xd, yd, zd = (
                    member(i, target, coset[i] ^ flips[i], (k >> (2 - i)) & 1) for i in range(3)
                )
                block = table_ref[((xd >> 1) * 4 + zd) * 2 + target]
                row = (yd * 2 + (xd & 1)) * ROWS
                tiles = STREAM_TILES[stream]
                for pair in range(tiles[0] // 2, tiles[-1] // 2 + 1):
                    start = pl.multiple_of(row + (pair // 4) * 16, 16)
                    col = (pair % 4) * 128
                    value = blocks[0, block, pl.ds(start, 16), col : col + 128]
                    value = value.astype(jnp.float32)
                    for i in range(2):
                        if 2 * pair + i in tiles:
                            out[k, 2 * pair + i - offset] = value[8 * i : 8 * i + 8]
        return carry

    count = sum(len(streams) for _, _, streams in parts)
    lax.fori_loop(0, 32, body, 0, unroll=4 if count == 1 else 1)


def pack(name, parts, table, grads, matrices=()):
    extra = [jax.ShapeDtypeStruct((ORDER, ORDER), kind) for kind in ROOT_KINDS] if matrices else []
    packed = [
        jax.ShapeDtypeStruct((32, sum(len(STREAM_TILES[s]) for s in streams), 8, 128), jnp.float32)
        for _, _, streams in parts
    ]
    return pl.pallas_call(
        functools.partial(pack_kernel, parts),
        out_shape=extra + packed,
        in_specs=[pl.BlockSpec(memory_space=pltpu.SMEM)] + whole(1 + len(matrices)),
        out_specs=whole(len(extra) + len(parts)),
        compiler_params=pltpu.CompilerParams(vmem_limit_bytes=VMEM_LIMIT),
        name=name,
    )(table, grads, *matrices)


def cost(products, moved):
    return pl.CostEstimate(
        flops=6 * products * ORDER**3, bytes_accessed=moved, transcendentals=0
    )


HALF, FULL = jnp.bfloat16, jnp.float32
ROOT_KINDS = (FULL, HALF, HALF, FULL, HALF, HALF, HALF, HALF)


def roots_kernel(ls_ref, rs_ref, lr_ref, rr_ref, *outs):
    for stat_ref, root_ref, refs in ((ls_ref, lr_ref, outs[:3]), (rs_ref, rr_ref, outs[3:])):
        root = root_ref[0]
        parts = split(root)
        square = split(product(parts, parts))
        fourth = split(product(square, square))
        fifth = product(parts, fourth)
        base = 1.25 * root - (DECAY / 4.0) * product(split(fifth), split(stat_ref[0]))
        refs[0][...] = base
        refs[1][...], refs[2][...] = split(fifth * ((1.0 - DECAY) / 4.0))
        if len(refs) > 3:
            refs[3][...], refs[4][...] = split(base)


def whole(count):
    return [pl.BlockSpec(memory_space=pltpu.VMEM)] * count


def join_kernel(k0, r0, k1, r1, k2, r2, out):
    for tiles, kept, got in zip(STREAM_TILES, (k0, k1, k2), (r0, r1, r2)):
        out[:, tiles[0] : tiles[-1] + 1] = kept[...] + got[...]


def join(pieces):
    return pl.pallas_call(
        join_kernel,
        out_shape=jax.ShapeDtypeStruct((8, 32, 8, 128), jnp.float32),
        in_specs=whole(6),
        out_specs=pl.BlockSpec(memory_space=pltpu.VMEM),
        compiler_params=pltpu.CompilerParams(vmem_limit_bytes=SMALL_LIMIT),
        name="join",
    )(*pieces)


def total_kernel(parts, out):
    value = parts[0]
    for i in range(1, 8):
        value = value + parts[i]
    for i in range(8):
        out[i] = value


def total(parts):
    return pl.pallas_call(
        total_kernel,
        out_shape=jax.ShapeDtypeStruct((8, 32, 8, 128), jnp.float32),
        in_specs=whole(1),
        out_specs=pl.BlockSpec(memory_space=pltpu.VMEM),
        compiler_params=pltpu.CompilerParams(vmem_limit_bytes=SMALL_LIMIT),
        name="total",
    )(parts)


def assemble(pieces, grad):
    for n in range(8):
        for pair in range(16):
            row = n * ROWS + (pair // 4) * 16
            col = (pair % 4) * 128
            grad[row : row + 16, col : col + 128] = pieces[n, 2 * pair : 2 * pair + 2].reshape(16, 128)


def rows_kernel(table_ref, pieces, lc, lkh, lkl, rkh, rkl, rch, rcl, out, grad):
    assemble(pieces, grad)
    g = split(grad[...])
    rows = pl.ds(pl.multiple_of(table_ref[20] * ROWS, ROWS), ROWS)
    inner = product((lkh[rows, :], lkl[rows, :]), g)
    left = lc[rows, :] - product(split(inner), g, NT)
    turned = split(product(split(left), g))
    inner = product(turned, (rkh[...], rkl[...]))
    inner = product(split(inner), g, NT)
    out[...] = product(turned, (rch[...], rcl[...])) - product(split(inner), g)


def precondition_rows(table, pieces, constants):
    return pl.pallas_call(
        rows_kernel,
        out_shape=jax.ShapeDtypeStruct((ROWS, ORDER), jnp.float32),
        in_specs=[pl.BlockSpec(memory_space=pltpu.SMEM)] + whole(8),
        out_specs=pl.BlockSpec(memory_space=pltpu.VMEM),
        scratch_shapes=[pltpu.VMEM((ORDER, ORDER), jnp.float32)],
        compiler_params=pltpu.CompilerParams(vmem_limit_bytes=VMEM_LIMIT),
        name="rows",
    )(table, pieces, *constants[:3], *constants[4:])


def stats_kernel(pieces, lc, lkh, lkl, rc, rkh, rkl, ls, rs, ln, rn, li, ri, grad):
    assemble(pieces, grad)
    g = split(grad[...])
    for dims, stat_ref, c_ref, kh, kl, new_ref, inv_ref in (
        (NT, ls, lc, lkh, lkl, ln, li),
        (TN, rs, rc, rkh, rkl, rn, ri),
    ):
        gram = product(g, g, dims)
        new_ref[0] = DECAY * stat_ref[0] + (1.0 - DECAY) * gram
        inv_ref[0] = c_ref[...] - product((kh[...], kl[...]), split(gram))


def statistics(pieces, constants, left_stat, right_stat):
    return pl.pallas_call(
        stats_kernel,
        out_shape=[jax.ShapeDtypeStruct((1, ORDER, ORDER), jnp.float32)] * 4,
        in_specs=whole(9),
        out_specs=whole(4),
        scratch_shapes=[pltpu.VMEM((ORDER, ORDER), jnp.float32)],
        compiler_params=pltpu.CompilerParams(vmem_limit_bytes=VMEM_LIMIT),
        cost_estimate=cost(4, 11 << 20),
        name="stats",
    )(pieces, *constants[:6], left_stat, right_stat)


def spread_kernel(table_ref, pair_ref, p0, p1, p2, p3, q0, q1, q2, q3, out, sems):
    xh, z, c = table_ref[16] >> 1, table_ref[18], table_ref[19]
    copies = []

    def put(src, xd, zd, cd):
        slot = (xd * 4 + zd) * 2 + cd
        copies.append(pltpu.make_async_copy(src, out.at[table_ref[slot]], sems.at[len(copies)]))

    for i in range(2):
        put(pair_ref.at[i], xh, z, c ^ i)
    put(p0, xh ^ 1, z, c)
    put(q0, xh ^ 1, z, 1 - c)
    for holder, group in ((c, (p1, p2, p3)), (1 - c, (q1, q2, q3))):
        for j, ref in enumerate(group):
            for i in range(2):
                put(ref.at[i], xh ^ holder, z ^ (j + 1), holder ^ i)
    for copy in copies:
        copy.start()
    for copy in copies:
        copy.wait()


def spread(table, pieces):
    return pl.pallas_call(
        spread_kernel,
        out_shape=jax.ShapeDtypeStruct((16, ROWS, ORDER), jnp.float32),
        in_specs=[pl.BlockSpec(memory_space=pltpu.SMEM)] + whole(9),
        out_specs=pl.BlockSpec(memory_space=pl.ANY),
        scratch_shapes=[pltpu.SemaphoreType.DMA((16,))],
        compiler_params=pltpu.CompilerParams(vmem_limit_bytes=SMALL_LIMIT),
        name="spread",
    )(table, *pieces)


def local(replica_grads, owner_table, left_stat, right_stat, left_root, right_root):
    x, y, z, c = place()
    slots = jnp.arange(16, dtype=jnp.int32)
    block_of_slot = jnp.sum(
        jnp.where(owner_table[None, :] == slots[:, None], slots[None, :], 0), axis=1
    )
    coords = jnp.stack([x, y, z, c, y * 2 + (x & 1)]).astype(jnp.int32)
    table = jnp.concatenate([block_of_slot, coords])
    streams = range(3)
    everything = tuple(streams)
    (first,) = pack("other0", [(False, 1, (0,))], table, replica_grads)
    table, first = lax.optimization_barrier((table, first))
    later = pack("other12", [(False, 1, (1,)), (False, 1, (2,))], table, replica_grads)
    table, later = lax.optimization_barrier((table, later))
    arrived = [send(value, CORE_SWAP) for value in (first, *later)]
    *mine, other = pack(
        "own", [(True, 1, (s,)) for s in streams] + [(False, 0, everything)], table, replica_grads
    )
    outgoing = [mine[s] + arrived[s] for s in streams]
    other, outgoing = lax.optimization_barrier((other, outgoing))
    table, other = lax.optimization_barrier((table, other))
    *constants, mine = pack(
        "keep",
        [(True, 0, everything)],
        table,
        replica_grads,
        (left_stat, right_stat, left_root, right_root),
    )
    arrived = send(other, CORE_SWAP)
    kept = [
        mine[:, tiles[0] : tiles[-1] + 1] + arrived[:, tiles[0] : tiles[-1] + 1]
        for tiles in STREAM_TILES
    ]
    tails = [None] * 3
    for step in range(3):
        for s in streams:
            axis = (s + step) % 3
            got = send(outgoing[s], axis_move(axis, first_masks(axis)))
            if step == 2:
                tails[s] = (kept[s], got)
                continue
            half = kept[s].shape[0] // 2
            outgoing[s] = kept[s][half:] + got[half:]
            kept[s] = kept[s][:half] + got[:half]
    joined = join([value for pair in tails for value in pair])
    parts = lax.all_to_all(joined, AXES, 0, 0, axis_index_groups=CUBES, tiled=True)
    pieces = lax.all_to_all(total(parts), ("y", "xl"), 0, 0, tiled=True)
    rows = precondition_rows(table, pieces, constants)
    both = jnp.stack([rows, send(rows, CORE_SWAP)])
    got = [None] * 4
    for j in (2, 1, 3):
        got[j] = send(both, permutation(lambda x, y, z, c, j=j: (x ^ (2 * c), y, z ^ j, c)))
    got[0] = send(rows, axis_move(0, (2, 2)))
    stats = statistics(pieces, constants, left_stat, right_stat)
    got, stats = lax.optimization_barrier((got, stats))
    swapped = [send(value, CORE_SWAP) for value in got]
    directions = spread(table, [both] + got + swapped)
    return (directions, *stats)


def solution(mesh):
    fine = Mesh(mesh.devices.reshape(SIZES), AXES)
    wide = ("xh", "z", "core")
    narrow = ("y", "xl")
    slot = P(wide, None, None)
    return jax.shard_map(
        local,
        mesh=fine,
        in_specs=(P(wide + narrow, None, None, None), P(), slot, slot, slot, slot),
        out_specs=(P(None, narrow, None), slot, slot, slot, slot),
        check_vma=False,
    )
```

```python
import functools

import jax
import jax.numpy as jnp
from jax import lax
from jax.experimental import pallas as pl
from jax.experimental.pallas import tpu as pltpu
from jax.sharding import Mesh, PartitionSpec as P

AXES = ("xh", "z", "core", "y", "xl")
SIZES = (2, 4, 2, 4, 2)
DECAY = 0.95
ORDER = 512
ROWS = 64
VMEM_LIMIT = 20 * 1024 * 1024
SMALL_LIMIT = 8 * 1024 * 1024
STREAM_TILES = (range(0, 11), range(11, 22), range(22, 32))


def index_of(x, y, z, c):
    return ((((x >> 1) * 4 + z) * 2 + c) * 4 + y) * 2 + (x & 1)


def permutation(move):
    return [
        (index_of(x, y, z, c), index_of(*move(x, y, z, c)))
        for x in range(4)
        for y in range(4)
        for z in range(4)
        for c in range(2)
    ]


def axis_move(axis, masks):
    def move(x, y, z, c):
        place = [x, y, z]
        place[axis] ^= masks[c]
        return (*place, c)

    return permutation(move)


CORE_SWAP = permutation(lambda x, y, z, c: (x, y, z, 1 - c))


FLIP = (0, 0, 1)


def member(axis, core, coset, bit):
    variant = core ^ FLIP[axis]
    return (1 - variant) * ((bit << 1) | (bit ^ coset)) + variant * ((coset << 1) | bit)


def coset_of(axis, core, position):
    variant = core ^ FLIP[axis]
    return (1 - variant) * ((position ^ (position >> 1)) & 1) + variant * (position >> 1)


def first_masks(axis):
    return tuple(1 + 2 * (core ^ FLIP[axis]) for core in range(2))


BITS = (0, 1)
CUBES = [
    [
        index_of(member(0, c, qx, vx), member(1, c, qy, vy), member(2, c, qz, vz), c)
        for vx in BITS
        for vy in BITS
        for vz in BITS
    ]
    for c in BITS
    for qx in BITS
    for qy in BITS
    for qz in BITS
]


def send(value, pairs):
    return lax.ppermute(value, AXES, pairs)


def place():
    xl = lax.axis_index("xl")
    x = lax.axis_index("xh") * 2 + xl
    return x, lax.axis_index("y"), lax.axis_index("z"), lax.axis_index("core")


def split(value):
    high = value.astype(jnp.bfloat16)
    low = (value - high.astype(jnp.float32)).astype(jnp.bfloat16)
    return high, low


def product(first, second, dims=((1,), (0,))):
    fh, fl = first
    sh, sl = second

    def dot(a, b):
        return lax.dot_general(a, b, (dims, ((), ())), preferred_element_type=jnp.float32)

    return dot(fh, sh) + (dot(fh, sl) + dot(fl, sh))


def thin_product(first, second, dims=((1,), (0,))):
    fh, fl = first
    sh, sl = second
    count = fh.shape[0]

    def dot(a, b):
        return lax.dot_general(a, b, (dims, ((), ())), preferred_element_type=jnp.float32)

    stacked = dot(jnp.concatenate([fh, fl], axis=0), sh)
    return stacked[:count] + (stacked[count:] + dot(fh, sl))


NT = ((1,), (1,))
TN = ((0,), (0,))


def pack_kernel(parts, table_ref, blocks, *rest):
    extra, outs = rest[: -len(parts)], rest[-len(parts) :]
    if extra:
        roots_kernel(*extra)
    here = [table_ref[16 + i] for i in range(3)]
    c = table_ref[19]
    targets = [c if own else 1 - c for own, _, _ in parts]
    cosets = [[coset_of(i, target, here[i]) for i in range(3)] for target in targets]

    def body(k, carry):
        for (_, half, streams), target, coset, out in zip(parts, targets, cosets, outs):
            offset = STREAM_TILES[streams[0]][0]
            for stream in streams:
                flips = [0, 0, 0]
                flips[stream] = half
                flips[(stream + 1) % 3] = (k >> 4) & 1
                flips[(stream + 2) % 3] = (k >> 3) & 1
                xd, yd, zd = (
                    member(i, target, coset[i] ^ flips[i], (k >> (2 - i)) & 1) for i in range(3)
                )
                block = table_ref[((xd >> 1) * 4 + zd) * 2 + target]
                row = (yd * 2 + (xd & 1)) * ROWS
                tiles = STREAM_TILES[stream]
                for pair in range(tiles[0] // 2, tiles[-1] // 2 + 1):
                    start = pl.multiple_of(row + (pair // 4) * 16, 16)
                    col = (pair % 4) * 128
                    value = blocks[0, block, pl.ds(start, 16), col : col + 128]
                    value = value.astype(jnp.float32)
                    for i in range(2):
                        if 2 * pair + i in tiles:
                            out[k, 2 * pair + i - offset] = value[8 * i : 8 * i + 8]
        return carry

    count = sum(len(streams) for _, _, streams in parts)
    lax.fori_loop(0, 32, body, 0, unroll=4 if count == 1 else 1)


def pack(name, parts, table, grads, matrices=()):
    extra = [jax.ShapeDtypeStruct((ORDER, ORDER), kind) for kind in ROOT_KINDS] if matrices else []
    packed = [
        jax.ShapeDtypeStruct((32, sum(len(STREAM_TILES[s]) for s in streams), 8, 128), jnp.float32)
        for _, _, streams in parts
    ]
    return pl.pallas_call(
        functools.partial(pack_kernel, parts),
        out_shape=extra + packed,
        in_specs=[pl.BlockSpec(memory_space=pltpu.SMEM)] + whole(1 + len(matrices)),
        out_specs=whole(len(extra) + len(parts)),
        compiler_params=pltpu.CompilerParams(vmem_limit_bytes=VMEM_LIMIT),
        name=name,
    )(table, grads, *matrices)


def cost(products, moved):
    return pl.CostEstimate(
        flops=6 * products * ORDER**3, bytes_accessed=moved, transcendentals=0
    )


HALF, FULL = jnp.bfloat16, jnp.float32
ROOT_KINDS = (FULL, HALF, HALF, FULL, HALF, HALF, HALF, HALF)


def roots_kernel(ls_ref, rs_ref, lr_ref, rr_ref, *outs):
    for stat_ref, root_ref, refs in ((ls_ref, lr_ref, outs[:3]), (rs_ref, rr_ref, outs[3:])):
        root = root_ref[0]
        parts = split(root)
        square = split(product(parts, parts))
        fourth = split(product(square, square))
        fifth = product(parts, fourth)
        base = 1.25 * root - (DECAY / 4.0) * product(split(fifth), split(stat_ref[0]))
        refs[0][...] = base
        refs[1][...], refs[2][...] = split(fifth * ((1.0 - DECAY) / 4.0))
        if len(refs) > 3:
            refs[3][...], refs[4][...] = split(base)


def whole(count):
    return [pl.BlockSpec(memory_space=pltpu.VMEM)] * count


def join_kernel(k0, r0, k1, r1, k2, r2, out):
    for tiles, kept, got in zip(STREAM_TILES, (k0, k1, k2), (r0, r1, r2)):
        out[:, tiles[0] : tiles[-1] + 1] = kept[...] + got[...]


def join(pieces):
    return pl.pallas_call(
        join_kernel,
        out_shape=jax.ShapeDtypeStruct((8, 32, 8, 128), jnp.float32),
        in_specs=whole(6),
        out_specs=pl.BlockSpec(memory_space=pltpu.VMEM),
        compiler_params=pltpu.CompilerParams(vmem_limit_bytes=SMALL_LIMIT),
        name="join",
    )(*pieces)


def total_kernel(parts, out):
    value = parts[0]
    for i in range(1, 8):
        value = value + parts[i]
    for i in range(8):
        out[i] = value


def total(parts):
    return pl.pallas_call(
        total_kernel,
        out_shape=jax.ShapeDtypeStruct((8, 32, 8, 128), jnp.float32),
        in_specs=whole(1),
        out_specs=pl.BlockSpec(memory_space=pltpu.VMEM),
        compiler_params=pltpu.CompilerParams(vmem_limit_bytes=SMALL_LIMIT),
        name="total",
    )(parts)


def assemble(pieces, grad):
    for n in range(8):
        for pair in range(16):
            row = n * ROWS + (pair // 4) * 16
            col = (pair % 4) * 128
            grad[row : row + 16, col : col + 128] = pieces[n, 2 * pair : 2 * pair + 2].reshape(16, 128)


def rows_kernel(table_ref, pieces, lc, lkh, lkl, rkh, rkl, rch, rcl, out, grad):
    assemble(pieces, grad)
    g = split(grad[...])
    rows = pl.ds(pl.multiple_of(table_ref[20] * ROWS, ROWS), ROWS)
    inner = thin_product((lkh[rows, :], lkl[rows, :]), g)
    left = lc[rows, :] - thin_product(split(inner), g, NT)
    turned = split(thin_product(split(left), g))
    inner = thin_product(turned, (rkh[...], rkl[...]))
    inner = thin_product(split(inner), g, NT)
    value = thin_product(turned, (rch[...], rcl[...])) - thin_product(split(inner), g)
    for i in range(8):
        out[i] = value


def precondition_rows(table, pieces, constants):
    return pl.pallas_call(
        rows_kernel,
        out_shape=jax.ShapeDtypeStruct((8, ROWS, ORDER), jnp.float32),
        in_specs=[pl.BlockSpec(memory_space=pltpu.SMEM)] + whole(8),
        out_specs=pl.BlockSpec(memory_space=pltpu.VMEM),
        scratch_shapes=[pltpu.VMEM((ORDER, ORDER), jnp.float32)],
        compiler_params=pltpu.CompilerParams(vmem_limit_bytes=VMEM_LIMIT),
        name="rows",
    )(table, pieces, *constants[:3], *constants[4:])


def stats_kernel(pieces, lc, lkh, lkl, rc, rkh, rkl, ls, rs, ln, rn, li, ri, grad):
    assemble(pieces, grad)
    g = split(grad[...])
    for dims, stat_ref, c_ref, kh, kl, new_ref, inv_ref in (
        (NT, ls, lc, lkh, lkl, ln, li),
        (TN, rs, rc, rkh, rkl, rn, ri),
    ):
        gram = product(g, g, dims)
        new_ref[0] = DECAY * stat_ref[0] + (1.0 - DECAY) * gram
        inv_ref[0] = c_ref[...] - product((kh[...], kl[...]), split(gram))


def statistics(pieces, constants, left_stat, right_stat):
    return pl.pallas_call(
        stats_kernel,
        out_shape=[jax.ShapeDtypeStruct((1, ORDER, ORDER), jnp.float32)] * 4,
        in_specs=whole(9),
        out_specs=whole(4),
        scratch_shapes=[pltpu.VMEM((ORDER, ORDER), jnp.float32)],
        compiler_params=pltpu.CompilerParams(vmem_limit_bytes=VMEM_LIMIT),
        cost_estimate=cost(4, 11 << 20),
        name="stats",
    )(pieces, *constants[:6], left_stat, right_stat)


def spread_kernel(late, table_ref, *refs):
    source, (out, sems) = refs[0], refs[-2:]
    core = 1 - table_ref[19] if late else table_ref[19]
    copies = [
        pltpu.make_async_copy(source.at[i], out.at[table_ref[2 * i + core]], sems.at[i])
        for i in range(8)
    ]
    for copy in copies:
        copy.start()
    for copy in copies:
        copy.wait()


def spread(table, source, before=None):
    late = before is not None
    anywhere = pl.BlockSpec(memory_space=pl.ANY)
    return pl.pallas_call(
        functools.partial(spread_kernel, late),
        out_shape=jax.ShapeDtypeStruct((16, ROWS, ORDER), jnp.float32),
        in_specs=[pl.BlockSpec(memory_space=pltpu.SMEM)] + whole(1) + [anywhere] * late,
        out_specs=anywhere,
        scratch_shapes=[pltpu.SemaphoreType.DMA((8,))],
        input_output_aliases={2: 0} if late else {},
        compiler_params=pltpu.CompilerParams(vmem_limit_bytes=SMALL_LIMIT),
        name="spread_late" if late else "spread",
    )(table, source, *([before] if late else []))


def local(replica_grads, owner_table, left_stat, right_stat, left_root, right_root):
    x, y, z, c = place()
    slots = jnp.arange(16, dtype=jnp.int32)
    block_of_slot = jnp.sum(
        jnp.where(owner_table[None, :] == slots[:, None], slots[None, :], 0), axis=1
    )
    coords = jnp.stack([x, y, z, c, y * 2 + (x & 1)]).astype(jnp.int32)
    table = jnp.concatenate([block_of_slot, coords])
    streams = range(3)
    everything = tuple(streams)
    arrived = []
    for s in streams:
        (value,) = pack(f"other{s}", [(False, 1, (s,))], table, replica_grads)
        table, value = lax.optimization_barrier((table, value))
        arrived.append(send(value, CORE_SWAP))
    mine = pack("own", [(True, 1, (s,)) for s in streams], table, replica_grads)
    table, mine = lax.optimization_barrier((table, mine))
    (other,) = pack("otherkeep", [(False, 0, everything)], table, replica_grads)
    outgoing = [mine[s] + arrived[s] for s in streams]
    table, other, _ = lax.optimization_barrier((table, other, outgoing))
    *constants, mine = pack(
        "keep",
        [(True, 0, everything)],
        table,
        replica_grads,
        (left_stat, right_stat, left_root, right_root),
    )
    arrived = send(other, CORE_SWAP)
    kept = [
        mine[:, tiles[0] : tiles[-1] + 1] + arrived[:, tiles[0] : tiles[-1] + 1]
        for tiles in STREAM_TILES
    ]
    tails = [None] * 3
    for step in range(3):
        for s in streams:
            axis = (s + step) % 3
            got = send(outgoing[s], axis_move(axis, first_masks(axis)))
            if step == 2:
                tails[s] = (kept[s], got)
                continue
            half = kept[s].shape[0] // 2
            outgoing[s] = kept[s][half:] + got[half:]
            kept[s] = kept[s][:half] + got[:half]
    joined = join([value for pair in tails for value in pair])
    parts = lax.all_to_all(joined, AXES, 0, 0, axis_index_groups=CUBES, tiled=True)
    pieces = lax.all_to_all(total(parts), ("y", "xl"), 0, 0, tiled=True)
    rows = precondition_rows(table, pieces, constants)
    got = lax.all_to_all(rows, ("xh", "z"), 0, 0, tiled=True)
    stats = statistics(pieces, constants, left_stat, right_stat)
    got, stats = lax.optimization_barrier((got, stats))
    swapped = send(got, CORE_SWAP)
    directions = spread(table, swapped, spread(table, got))
    return (directions, *stats)


def solution(mesh):
    fine = Mesh(mesh.devices.reshape(SIZES), AXES)
    wide = ("xh", "z", "core")
    narrow = ("y", "xl")
    slot = P(wide, None, None)
    return jax.shard_map(
        local,
        mesh=fine,
        in_specs=(P(wide + narrow, None, None, None), P(), slot, slot, slot, slot),
        out_specs=(P(None, narrow, None), slot, slot, slot, slot),
        check_vma=False,
    )
```

```python
import functools

import jax
import jax.numpy as jnp
from jax import lax
from jax.experimental import pallas as pl
from jax.experimental.pallas import tpu as pltpu
from jax.sharding import Mesh, PartitionSpec as P

AXES = ("xh", "z", "core", "y", "xl")
SIZES = (2, 4, 2, 4, 2)
DECAY = 0.95
ORDER = 512
ROWS = 64
VMEM_LIMIT = 20 * 1024 * 1024
SMALL_LIMIT = 8 * 1024 * 1024
STREAM_TILES = (range(0, 11), range(11, 22), range(22, 32))


def index_of(x, y, z, c):
    return ((((x >> 1) * 4 + z) * 2 + c) * 4 + y) * 2 + (x & 1)


def permutation(move):
    return [
        (index_of(x, y, z, c), index_of(*move(x, y, z, c)))
        for x in range(4)
        for y in range(4)
        for z in range(4)
        for c in range(2)
    ]


def axis_move(axis, masks):
    def move(x, y, z, c):
        place = [x, y, z]
        place[axis] ^= masks[c]
        return (*place, c)

    return permutation(move)


CORE_SWAP = permutation(lambda x, y, z, c: (x, y, z, 1 - c))


FLIP = (0, 0, 1)


def member(axis, core, coset, bit):
    variant = core ^ FLIP[axis]
    return (1 - variant) * ((bit << 1) | (bit ^ coset)) + variant * ((coset << 1) | bit)


def coset_of(axis, core, position):
    variant = core ^ FLIP[axis]
    return (1 - variant) * ((position ^ (position >> 1)) & 1) + variant * (position >> 1)


def first_masks(axis):
    return tuple(1 + 2 * (core ^ FLIP[axis]) for core in range(2))


BITS = (0, 1)
CUBES = [
    [
        index_of(member(0, c, qx, vx), member(1, c, qy, vy), member(2, c, qz, vz), c)
        for vx in BITS[::-1]
        for vy in BITS[::-1]
        for vz in BITS[::-1]
    ]
    for c in BITS
    for qx in BITS
    for qy in BITS
    for qz in BITS
]


def send(value, pairs):
    return lax.ppermute(value, AXES, pairs)


def place():
    xl = lax.axis_index("xl")
    x = lax.axis_index("xh") * 2 + xl
    return x, lax.axis_index("y"), lax.axis_index("z"), lax.axis_index("core")


def split(value):
    high = value.astype(jnp.bfloat16)
    low = (value - high.astype(jnp.float32)).astype(jnp.bfloat16)
    return high, low


def product(first, second, dims=((1,), (0,))):
    fh, fl = first
    sh, sl = second

    def dot(a, b):
        return lax.dot_general(a, b, (dims, ((), ())), preferred_element_type=jnp.float32)

    return dot(fh, sh) + (dot(fh, sl) + dot(fl, sh))


def thin_product(first, second, dims=((1,), (0,))):
    fh, fl = first
    sh, sl = second
    count = fh.shape[0]

    def dot(a, b):
        return lax.dot_general(a, b, (dims, ((), ())), preferred_element_type=jnp.float32)

    stacked = dot(jnp.concatenate([fh, fl], axis=0), sh)
    return stacked[:count] + (stacked[count:] + dot(fh, sl))


NT = ((1,), (1,))
TN = ((0,), (0,))


def pack_kernel(parts, table_ref, blocks, *rest):
    extra, outs = rest[: -len(parts)], rest[-len(parts) :]
    if extra:
        roots_kernel(*extra)
    here = [table_ref[16 + i] for i in range(3)]
    c = table_ref[19]
    targets = [c if own else 1 - c for own, _, _ in parts]
    cosets = [[coset_of(i, target, here[i]) for i in range(3)] for target in targets]

    def body(k, carry):
        for (_, half, streams), target, coset, out in zip(parts, targets, cosets, outs):
            offset = STREAM_TILES[streams[0]][0]
            for stream in streams:
                flips = [0, 0, 0]
                flips[stream] = half
                flips[(stream + 1) % 3] = (k >> 4) & 1
                flips[(stream + 2) % 3] = (k >> 3) & 1
                xd, yd, zd = (
                    member(i, target, coset[i] ^ flips[i], 1 - ((k >> (2 - i)) & 1)) for i in range(3)
                )
                block = table_ref[((xd >> 1) * 4 + zd) * 2 + target]
                row = (yd * 2 + (xd & 1)) * ROWS
                tiles = STREAM_TILES[stream]
                for pair in range(tiles[0] // 2, tiles[-1] // 2 + 1):
                    start = pl.multiple_of(row + (pair // 4) * 16, 16)
                    col = (pair % 4) * 128
                    value = blocks[0, block, pl.ds(start, 16), col : col + 128]
                    value = value.astype(jnp.float32)
                    for i in range(2):
                        if 2 * pair + i in tiles:
                            out[k, 2 * pair + i - offset] = value[8 * i : 8 * i + 8]
        return carry

    count = sum(len(streams) for _, _, streams in parts)
    lax.fori_loop(0, 32, body, 0, unroll=8 if count == 1 else 2)


def pack(name, parts, table, grads, matrices=()):
    extra = [jax.ShapeDtypeStruct((ORDER, ORDER), kind) for kind in ROOT_KINDS] if matrices else []
    packed = [
        jax.ShapeDtypeStruct((32, sum(len(STREAM_TILES[s]) for s in streams), 8, 128), jnp.float32)
        for _, _, streams in parts
    ]
    return pl.pallas_call(
        functools.partial(pack_kernel, parts),
        out_shape=extra + packed,
        in_specs=[pl.BlockSpec(memory_space=pltpu.SMEM)] + whole(1 + len(matrices)),
        out_specs=whole(len(extra) + len(parts)),
        compiler_params=pltpu.CompilerParams(vmem_limit_bytes=VMEM_LIMIT),
        name=name,
    )(table, grads, *matrices)


def cost(products, moved):
    return pl.CostEstimate(
        flops=6 * products * ORDER**3, bytes_accessed=moved, transcendentals=0
    )


HALF, FULL = jnp.bfloat16, jnp.float32
ROOT_KINDS = (FULL, HALF, HALF, FULL, HALF, HALF, HALF, HALF)


def roots_kernel(ls_ref, rs_ref, lr_ref, rr_ref, *outs):
    for stat_ref, root_ref, refs in ((ls_ref, lr_ref, outs[:3]), (rs_ref, rr_ref, outs[3:])):
        root = root_ref[0]
        parts = split(root)
        square = split(product(parts, parts))
        fourth = split(product(square, square))
        fifth = product(parts, fourth)
        base = 1.25 * root - (DECAY / 4.0) * product(split(fifth), split(stat_ref[0]))
        refs[0][...] = base
        refs[1][...], refs[2][...] = split(fifth * ((1.0 - DECAY) / 4.0))
        if len(refs) > 3:
            refs[3][...], refs[4][...] = split(base)


def whole(count):
    return [pl.BlockSpec(memory_space=pltpu.VMEM)] * count


def join_kernel(k0, r0, k1, r1, k2, r2, out):
    for tiles, kept, got in zip(STREAM_TILES, (k0, k1, k2), (r0, r1, r2)):
        out[:, tiles[0] : tiles[-1] + 1] = kept[...] + got[...]


def join(pieces):
    return pl.pallas_call(
        join_kernel,
        out_shape=jax.ShapeDtypeStruct((8, 32, 8, 128), jnp.float32),
        in_specs=whole(6),
        out_specs=pl.BlockSpec(memory_space=pltpu.VMEM),
        compiler_params=pltpu.CompilerParams(vmem_limit_bytes=SMALL_LIMIT),
        name="join",
    )(*pieces)


def total_kernel(parts, out):
    for tile in range(32):
        value = parts[0, tile]
        for i in range(1, 8):
            value = value + parts[i, tile]
        row, col = tile // 8 * 16 + tile % 2 * 8, tile // 2 % 4 * 128
        for i in range(8):
            out[i, row : row + 8, col : col + 128] = value


def total(parts):
    return pl.pallas_call(
        total_kernel,
        out_shape=jax.ShapeDtypeStruct((8, ROWS, ORDER), jnp.float32),
        in_specs=whole(1),
        out_specs=pl.BlockSpec(memory_space=pltpu.VMEM),
        compiler_params=pltpu.CompilerParams(vmem_limit_bytes=SMALL_LIMIT),
        name="total",
    )(parts)


def rows_kernel(table_ref, grad, lc, lkh, lkl, rkh, rkl, rch, rcl, out):
    g = split(grad[...])
    rows = pl.ds(pl.multiple_of(table_ref[20] * ROWS, ROWS), ROWS)
    inner = thin_product((lkh[rows, :], lkl[rows, :]), g)
    left = lc[rows, :] - thin_product(split(inner), g, NT)
    turned = split(thin_product(split(left), g))
    inner = thin_product(turned, (rkh[...], rkl[...]))
    inner = thin_product(split(inner), g, NT)
    value = thin_product(turned, (rch[...], rcl[...])) - thin_product(split(inner), g)
    for i in range(8):
        out[i] = value


def precondition_rows(table, grad, constants):
    return pl.pallas_call(
        rows_kernel,
        out_shape=jax.ShapeDtypeStruct((8, ROWS, ORDER), jnp.float32),
        in_specs=[pl.BlockSpec(memory_space=pltpu.SMEM)] + whole(8),
        out_specs=pl.BlockSpec(memory_space=pltpu.VMEM),
        compiler_params=pltpu.CompilerParams(vmem_limit_bytes=VMEM_LIMIT),
        name="rows",
    )(table, grad, *constants[:3], *constants[4:])


def stats_kernel(grad, lc, lkh, lkl, rc, rkh, rkl, ls, rs, ln, rn, li, ri):
    g = split(grad[...])
    for dims, stat_ref, c_ref, kh, kl, new_ref, inv_ref in (
        (NT, ls, lc, lkh, lkl, ln, li),
        (TN, rs, rc, rkh, rkl, rn, ri),
    ):
        gram = product(g, g, dims)
        new_ref[0] = DECAY * stat_ref[0] + (1.0 - DECAY) * gram
        inv_ref[0] = c_ref[...] - product((kh[...], kl[...]), split(gram))


def statistics(grad, constants, left_stat, right_stat):
    return pl.pallas_call(
        stats_kernel,
        out_shape=[jax.ShapeDtypeStruct((1, ORDER, ORDER), jnp.float32)] * 4,
        in_specs=whole(9),
        out_specs=whole(4),
        compiler_params=pltpu.CompilerParams(vmem_limit_bytes=VMEM_LIMIT),
        cost_estimate=cost(4, 11 << 20),
        name="stats",
    )(grad, *constants[:6], left_stat, right_stat)


def spread_kernel(late, table_ref, *refs):
    source, (out, sems) = refs[0], refs[-2:]
    core = 1 - table_ref[19] if late else table_ref[19]
    copies = [
        pltpu.make_async_copy(source.at[i], out.at[table_ref[2 * i + core]], sems.at[i])
        for i in range(8)
    ]
    for copy in copies:
        copy.start()
    for copy in copies:
        copy.wait()


def spread(table, source, before=None):
    late = before is not None
    anywhere = pl.BlockSpec(memory_space=pl.ANY)
    return pl.pallas_call(
        functools.partial(spread_kernel, late),
        out_shape=jax.ShapeDtypeStruct((16, ROWS, ORDER), jnp.float32),
        in_specs=[pl.BlockSpec(memory_space=pltpu.SMEM)] + whole(1) + [anywhere] * late,
        out_specs=anywhere,
        scratch_shapes=[pltpu.SemaphoreType.DMA((8,))],
        input_output_aliases={2: 0} if late else {},
        compiler_params=pltpu.CompilerParams(vmem_limit_bytes=SMALL_LIMIT),
        name="spread_late" if late else "spread",
    )(table, source, *([before] if late else []))


def local(replica_grads, owner_table, left_stat, right_stat, left_root, right_root):
    x, y, z, c = place()
    slots = jnp.arange(16, dtype=jnp.int32)
    block_of_slot = jnp.sum(
        jnp.where(owner_table[None, :] == slots[:, None], slots[None, :], 0), axis=1
    )
    coords = jnp.stack([x, y, z, c, y * 2 + (x & 1)]).astype(jnp.int32)
    table = jnp.concatenate([block_of_slot, coords])
    streams = range(3)
    everything = tuple(streams)
    arrived = []
    for s in streams:
        (value,) = pack(f"other{s}", [(False, 1, (s,))], table, replica_grads)
        table, value = lax.optimization_barrier((table, value))
        arrived.append(send(value, CORE_SWAP))
    mine = pack("own", [(True, 1, (s,)) for s in streams], table, replica_grads)
    table, mine = lax.optimization_barrier((table, mine))
    (other,) = pack("otherkeep", [(False, 0, everything)], table, replica_grads)
    outgoing = [mine[s] + arrived[s] for s in streams]
    table, other, _ = lax.optimization_barrier((table, other, outgoing))
    *constants, mine = pack(
        "keep",
        [(True, 0, everything)],
        table,
        replica_grads,
        (left_stat, right_stat, left_root, right_root),
    )
    arrived = send(other, CORE_SWAP)
    kept = [
        mine[:, tiles[0] : tiles[-1] + 1] + arrived[:, tiles[0] : tiles[-1] + 1]
        for tiles in STREAM_TILES
    ]
    tails = [None] * 3
    for step in range(3):
        for s in streams:
            axis = (s + step) % 3
            got = send(outgoing[s], axis_move(axis, first_masks(axis)))
            if step == 2:
                tails[s] = (kept[s], got)
                continue
            half = kept[s].shape[0] // 2
            outgoing[s] = kept[s][half:] + got[half:]
            kept[s] = kept[s][:half] + got[:half]
    joined = join([value for pair in tails for value in pair])
    parts = lax.all_to_all(joined, AXES, 0, 0, axis_index_groups=CUBES, tiled=True)
    grad = lax.all_to_all(total(parts), ("y", "xl"), 0, 0, tiled=True).reshape(ORDER, ORDER)
    rows = precondition_rows(table, grad, constants)
    got = lax.all_to_all(rows, ("xh", "z"), 0, 0, tiled=True)
    stats = statistics(grad, constants, left_stat, right_stat)
    got, stats = lax.optimization_barrier((got, stats))
    swapped = send(got, CORE_SWAP)
    directions = spread(table, swapped, spread(table, got))
    return (directions, *stats)


def solution(mesh):
    fine = Mesh(mesh.devices.reshape(SIZES), AXES)
    wide = ("xh", "z", "core")
    narrow = ("y", "xl")
    slot = P(wide, None, None)
    return jax.shard_map(
        local,
        mesh=fine,
        in_specs=(P(wide + narrow, None, None, None), P(), slot, slot, slot, slot),
        out_specs=(P(None, narrow, None), slot, slot, slot, slot),
        check_vma=False,
    )
```

```python
import functools

import jax
import jax.numpy as jnp
from jax import lax
from jax.experimental import pallas as pl
from jax.experimental.pallas import tpu as pltpu
from jax.sharding import Mesh, PartitionSpec as P

AXES = ("xh", "z", "core", "y", "xl")
SIZES = (2, 4, 2, 4, 2)
DECAY = 0.95
ORDER = 512
ROWS = 64
VMEM_LIMIT = 20 * 1024 * 1024
SMALL_LIMIT = 8 * 1024 * 1024
STREAM_TILES = (range(0, 11), range(11, 22), range(22, 32))


def index_of(x, y, z, c):
    return ((((x >> 1) * 4 + z) * 2 + c) * 4 + y) * 2 + (x & 1)


def permutation(move):
    return [
        (index_of(x, y, z, c), index_of(*move(x, y, z, c)))
        for x in range(4)
        for y in range(4)
        for z in range(4)
        for c in range(2)
    ]


def axis_move(axis, masks):
    def move(x, y, z, c):
        place = [x, y, z]
        place[axis] ^= masks[c]
        return (*place, c)

    return permutation(move)


CORE_SWAP = permutation(lambda x, y, z, c: (x, y, z, 1 - c))


FLIP = (0, 0, 1)


def member(axis, core, coset, bit):
    variant = core ^ FLIP[axis]
    return (1 - variant) * ((bit << 1) | (bit ^ coset)) + variant * ((coset << 1) | bit)


def coset_of(axis, core, position):
    variant = core ^ FLIP[axis]
    return (1 - variant) * ((position ^ (position >> 1)) & 1) + variant * (position >> 1)


def first_masks(axis):
    return tuple(1 + 2 * (core ^ FLIP[axis]) for core in range(2))


BITS = (0, 1)
CUBES = [
    [
        index_of(member(0, c, qx, vx), member(1, c, qy, vy), member(2, c, qz, vz), c)
        for vx in BITS[::-1]
        for vy in BITS[::-1]
        for vz in BITS[::-1]
    ]
    for c in BITS
    for qx in BITS
    for qy in BITS
    for qz in BITS
]


def send(value, pairs):
    return lax.ppermute(value, AXES, pairs)


def place():
    xl = lax.axis_index("xl")
    x = lax.axis_index("xh") * 2 + xl
    return x, lax.axis_index("y"), lax.axis_index("z"), lax.axis_index("core")


def split(value):
    high = value.astype(jnp.bfloat16)
    low = (value - high.astype(jnp.float32)).astype(jnp.bfloat16)
    return high, low


def product(first, second, dims=((1,), (0,))):
    fh, fl = first
    sh, sl = second

    def dot(a, b):
        return lax.dot_general(a, b, (dims, ((), ())), preferred_element_type=jnp.float32)

    return dot(fh, sh) + (dot(fh, sl) + dot(fl, sh))


def thin_product(first, second, dims=((1,), (0,))):
    fh, fl = first
    sh, sl = second
    count = fh.shape[0]

    def dot(a, b):
        return lax.dot_general(a, b, (dims, ((), ())), preferred_element_type=jnp.float32)

    stacked = dot(jnp.concatenate([fh, fl], axis=0), sh)
    return stacked[:count] + (stacked[count:] + dot(fh, sl))


NT = ((1,), (1,))
TN = ((0,), (0,))


def pack_kernel(parts, table_ref, blocks, *rest):
    extra, outs = rest[: -len(parts)], rest[-len(parts) :]
    if extra:
        roots_kernel(*extra)
    here = [table_ref[16 + i] for i in range(3)]
    c = table_ref[19]
    targets = [c if own else 1 - c for own, _, _ in parts]
    cosets = [[coset_of(i, target, here[i]) for i in range(3)] for target in targets]

    def body(k, carry):
        for (_, half, streams), target, coset, out in zip(parts, targets, cosets, outs):
            offset = STREAM_TILES[streams[0]][0]
            for stream in streams:
                flips = [0, 0, 0]
                flips[stream] = half
                flips[(stream + 1) % 3] = (k >> 4) & 1
                flips[(stream + 2) % 3] = (k >> 3) & 1
                xd, yd, zd = (
                    member(i, target, coset[i] ^ flips[i], 1 - ((k >> (2 - i)) & 1)) for i in range(3)
                )
                block = table_ref[((xd >> 1) * 4 + zd) * 2 + target]
                row = (yd * 2 + (xd & 1)) * ROWS
                tiles = STREAM_TILES[stream]
                for pair in range(tiles[0] // 2, tiles[-1] // 2 + 1):
                    start = pl.multiple_of(row + (pair // 4) * 16, 16)
                    col = (pair % 4) * 128
                    value = blocks[0, block, pl.ds(start, 16), col : col + 128]
                    value = value.astype(jnp.float32)
                    for i in range(2):
                        if 2 * pair + i in tiles:
                            out[k, 2 * pair + i - offset] = value[8 * i : 8 * i + 8]
        return carry

    count = sum(len(streams) for _, _, streams in parts)
    lax.fori_loop(0, 32, body, 0, unroll=8 if count == 1 else 2)


def pack(name, parts, table, grads, matrices=()):
    extra = [jax.ShapeDtypeStruct((ORDER, ORDER), kind) for kind in ROOT_KINDS] if matrices else []
    packed = [
        jax.ShapeDtypeStruct((32, sum(len(STREAM_TILES[s]) for s in streams), 8, 128), jnp.float32)
        for _, _, streams in parts
    ]
    return pl.pallas_call(
        functools.partial(pack_kernel, parts),
        out_shape=extra + packed,
        in_specs=[pl.BlockSpec(memory_space=pltpu.SMEM)] + whole(1 + len(matrices)),
        out_specs=whole(len(extra) + len(parts)),
        compiler_params=pltpu.CompilerParams(vmem_limit_bytes=VMEM_LIMIT),
        name=name,
    )(table, grads, *matrices)


def cost(products, moved):
    return pl.CostEstimate(
        flops=6 * products * ORDER**3, bytes_accessed=moved, transcendentals=0
    )


HALF, FULL = jnp.bfloat16, jnp.float32
ROOT_KINDS = (FULL, HALF, HALF, FULL, HALF, HALF, HALF, HALF)


def roots_kernel(ls_ref, rs_ref, lr_ref, rr_ref, *outs):
    for stat_ref, root_ref, refs in ((ls_ref, lr_ref, outs[:3]), (rs_ref, rr_ref, outs[3:])):
        root = root_ref[0]
        parts = split(root)
        square = split(product(parts, parts))
        fourth = split(product(square, square))
        fifth = product(parts, fourth)
        base = 1.25 * root - (DECAY / 4.0) * product(split(fifth), split(stat_ref[0]))
        refs[0][...] = base
        refs[1][...], refs[2][...] = split(fifth * ((1.0 - DECAY) / 4.0))
        if len(refs) > 3:
            refs[3][...], refs[4][...] = split(base)


def whole(count):
    return [pl.BlockSpec(memory_space=pltpu.VMEM)] * count


def join_kernel(k0, r0, k1, r1, k2, r2, out):
    for tiles, kept, got in zip(STREAM_TILES, (k0, k1, k2), (r0, r1, r2)):
        out[:, tiles[0] : tiles[-1] + 1] = kept[...] + got[...]


def join(pieces):
    return pl.pallas_call(
        join_kernel,
        out_shape=jax.ShapeDtypeStruct((8, 32, 8, 128), jnp.float32),
        in_specs=whole(6),
        out_specs=pl.BlockSpec(memory_space=pltpu.VMEM),
        compiler_params=pltpu.CompilerParams(vmem_limit_bytes=SMALL_LIMIT),
        name="join",
    )(*pieces)


def total_kernel(parts, out):
    for tile in range(32):
        value = parts[0, tile]
        for i in range(1, 8):
            value = value + parts[i, tile]
        row, col = tile // 8 * 16 + tile % 2 * 8, tile // 2 % 4 * 128
        for i in range(8):
            out[i, row : row + 8, col : col + 128] = value


def total(parts):
    return pl.pallas_call(
        total_kernel,
        out_shape=jax.ShapeDtypeStruct((8, ROWS, ORDER), jnp.float32),
        in_specs=whole(1),
        out_specs=pl.BlockSpec(memory_space=pltpu.VMEM),
        compiler_params=pltpu.CompilerParams(vmem_limit_bytes=SMALL_LIMIT),
        name="total",
    )(parts)


def rows_kernel(table_ref, grad, lc, lkh, lkl, rkh, rkl, rch, rcl, out, value, sems):
    g = split(grad[...])
    rows = pl.ds(pl.multiple_of(table_ref[20] * ROWS, ROWS), ROWS)
    inner = thin_product((lkh[rows, :], lkl[rows, :]), g)
    left = lc[rows, :] - thin_product(split(inner), g, NT)
    turned = split(thin_product(split(left), g))
    inner = thin_product(turned, (rkh[...], rkl[...]))
    inner = thin_product(split(inner), g, NT)
    inner = split(inner)
    copies = []
    for half in range(2):
        cols = slice(half * 256, half * 256 + 256)
        value[:, cols] = thin_product(turned, (rch[:, cols], rcl[:, cols])) - thin_product(
            inner, tuple(term[:, cols] for term in g)
        )
        for i in range(8):
            copies.append(
                pltpu.make_async_copy(
                    value.at[:, cols], out.at[i, :, cols], sems.at[8 * half + i]
                )
            )
            copies[-1].start()
    for copy in copies:
        copy.wait()


def precondition_rows(table, grad, constants):
    return pl.pallas_call(
        rows_kernel,
        out_shape=jax.ShapeDtypeStruct((8, ROWS, ORDER), jnp.float32),
        in_specs=[pl.BlockSpec(memory_space=pltpu.SMEM)] + whole(8),
        out_specs=pl.BlockSpec(memory_space=pl.ANY),
        scratch_shapes=[pltpu.VMEM((ROWS, ORDER), jnp.float32), pltpu.SemaphoreType.DMA((16,))],
        compiler_params=pltpu.CompilerParams(vmem_limit_bytes=VMEM_LIMIT),
        name="rows",
    )(table, grad, *constants[:3], *constants[4:])


def stats_kernel(grad, lc, lkh, lkl, rc, rkh, rkl, ls, rs, ln, rn, li, ri):
    g = split(grad[...])
    for dims, stat_ref, c_ref, kh, kl, new_ref, inv_ref in (
        (NT, ls, lc, lkh, lkl, ln, li),
        (TN, rs, rc, rkh, rkl, rn, ri),
    ):
        gram = product(g, g, dims)
        new_ref[0] = DECAY * stat_ref[0] + (1.0 - DECAY) * gram
        inv_ref[0] = c_ref[...] - product((kh[...], kl[...]), split(gram))


def statistics(grad, constants, left_stat, right_stat):
    return pl.pallas_call(
        stats_kernel,
        out_shape=[jax.ShapeDtypeStruct((1, ORDER, ORDER), jnp.float32)] * 4,
        in_specs=whole(9),
        out_specs=whole(4),
        compiler_params=pltpu.CompilerParams(vmem_limit_bytes=VMEM_LIMIT),
        cost_estimate=cost(4, 11 << 20),
        name="stats",
    )(grad, *constants[:6], left_stat, right_stat)


def spread_kernel(late, table_ref, *refs):
    source, (out, sems) = refs[0], refs[-2:]
    core = 1 - table_ref[19] if late else table_ref[19]
    copies = [
        pltpu.make_async_copy(source.at[i], out.at[table_ref[2 * i + core]], sems.at[i])
        for i in range(8)
    ]
    for copy in copies:
        copy.start()
    for copy in copies:
        copy.wait()


def spread(table, source, before=None):
    late = before is not None
    anywhere = pl.BlockSpec(memory_space=pl.ANY)
    return pl.pallas_call(
        functools.partial(spread_kernel, late),
        out_shape=jax.ShapeDtypeStruct((16, ROWS, ORDER), jnp.float32),
        in_specs=[pl.BlockSpec(memory_space=pltpu.SMEM)] + whole(1) + [anywhere] * late,
        out_specs=anywhere,
        scratch_shapes=[pltpu.SemaphoreType.DMA((8,))],
        input_output_aliases={2: 0} if late else {},
        compiler_params=pltpu.CompilerParams(vmem_limit_bytes=SMALL_LIMIT),
        name="spread_late" if late else "spread",
    )(table, source, *([before] if late else []))


def local(replica_grads, owner_table, left_stat, right_stat, left_root, right_root):
    x, y, z, c = place()
    slots = jnp.arange(16, dtype=jnp.int32)
    block_of_slot = jnp.sum(
        jnp.where(owner_table[None, :] == slots[:, None], slots[None, :], 0), axis=1
    )
    coords = jnp.stack([x, y, z, c, y * 2 + (x & 1)]).astype(jnp.int32)
    table = jnp.concatenate([block_of_slot, coords])
    streams = range(3)
    everything = tuple(streams)
    arrived = []
    for s in streams:
        (value,) = pack(f"other{s}", [(False, 1, (s,))], table, replica_grads)
        table, value = lax.optimization_barrier((table, value))
        arrived.append(send(value, CORE_SWAP))
    mine = pack("own", [(True, 1, (s,)) for s in streams], table, replica_grads)
    table, mine = lax.optimization_barrier((table, mine))
    (other,) = pack("otherkeep", [(False, 0, everything)], table, replica_grads)
    outgoing = [mine[s] + arrived[s] for s in streams]
    table, other, _ = lax.optimization_barrier((table, other, outgoing))
    *constants, mine = pack(
        "keep",
        [(True, 0, everything)],
        table,
        replica_grads,
        (left_stat, right_stat, left_root, right_root),
    )
    arrived = send(other, CORE_SWAP)
    kept = [
        mine[:, tiles[0] : tiles[-1] + 1] + arrived[:, tiles[0] : tiles[-1] + 1]
        for tiles in STREAM_TILES
    ]
    tails = [None] * 3
    for step in range(3):
        for s in streams:
            axis = (s + step) % 3
            got = send(outgoing[s], axis_move(axis, first_masks(axis)))
            if step == 2:
                tails[s] = (kept[s], got)
                continue
            half = kept[s].shape[0] // 2
            outgoing[s] = kept[s][half:] + got[half:]
            kept[s] = kept[s][:half] + got[:half]
    joined = join([value for pair in tails for value in pair])
    parts = lax.all_to_all(joined, AXES, 0, 0, axis_index_groups=CUBES, tiled=True)
    grad = lax.all_to_all(total(parts), ("y", "xl"), 0, 0, tiled=True).reshape(ORDER, ORDER)
    rows = precondition_rows(table, grad, constants)
    got = lax.all_to_all(rows, ("xh", "z"), 0, 0, tiled=True)
    stats = statistics(grad, constants, left_stat, right_stat)
    got, stats = lax.optimization_barrier((got, stats))
    swapped = send(got, CORE_SWAP)
    directions = spread(table, swapped, spread(table, got))
    return (directions, *stats)


def solution(mesh):
    fine = Mesh(mesh.devices.reshape(SIZES), AXES)
    wide = ("xh", "z", "core")
    narrow = ("y", "xl")
    slot = P(wide, None, None)
    return jax.shard_map(
        local,
        mesh=fine,
        in_specs=(P(wide + narrow, None, None, None), P(), slot, slot, slot, slot),
        out_specs=(P(None, narrow, None), slot, slot, slot, slot),
        check_vma=False,
    )
```

```python
import functools

import jax
import jax.numpy as jnp
from jax import lax
from jax.experimental import pallas as pl
from jax.experimental.pallas import tpu as pltpu
from jax.sharding import Mesh, PartitionSpec as P

AXES = ("xh", "z", "core", "y", "xl")
SIZES = (2, 4, 2, 4, 2)
DECAY = 0.95
ORDER = 512
ROWS = 64
VMEM_LIMIT = 20 * 1024 * 1024
SMALL_LIMIT = 8 * 1024 * 1024
STREAM_TILES = (range(0, 11), range(11, 22), range(22, 32))


def index_of(x, y, z, c):
    return ((((x >> 1) * 4 + z) * 2 + c) * 4 + y) * 2 + (x & 1)


def permutation(move):
    return [
        (index_of(x, y, z, c), index_of(*move(x, y, z, c)))
        for x in range(4)
        for y in range(4)
        for z in range(4)
        for c in range(2)
    ]


def axis_move(axis, masks):
    def move(x, y, z, c):
        place = [x, y, z]
        place[axis] ^= masks[c]
        return (*place, c)

    return permutation(move)


CORE_SWAP = permutation(lambda x, y, z, c: (x, y, z, 1 - c))


FLIP = (0, 0, 1)


def member(axis, core, coset, bit):
    variant = core ^ FLIP[axis]
    return (1 - variant) * ((bit << 1) | (bit ^ coset)) + variant * ((coset << 1) | bit)


def coset_of(axis, core, position):
    variant = core ^ FLIP[axis]
    return (1 - variant) * ((position ^ (position >> 1)) & 1) + variant * (position >> 1)


def first_masks(axis):
    return tuple(1 + 2 * (core ^ FLIP[axis]) for core in range(2))


BITS = (0, 1)
CUBES = [
    [
        index_of(member(0, c, qx, vx), member(1, c, qy, vy), member(2, c, qz, vz), c)
        for vx in BITS[::-1]
        for vy in BITS[::-1]
        for vz in BITS[::-1]
    ]
    for c in BITS
    for qx in BITS
    for qy in BITS
    for qz in BITS
]


def send(value, pairs):
    return lax.ppermute(value, AXES, pairs)


def place():
    xl = lax.axis_index("xl")
    x = lax.axis_index("xh") * 2 + xl
    return x, lax.axis_index("y"), lax.axis_index("z"), lax.axis_index("core")


def split(value):
    high = value.astype(jnp.bfloat16)
    low = (value - high.astype(jnp.float32)).astype(jnp.bfloat16)
    return high, low


def product(first, second, dims=((1,), (0,))):
    fh, fl = first
    sh, sl = second

    def dot(a, b):
        return lax.dot_general(a, b, (dims, ((), ())), preferred_element_type=jnp.float32)

    return dot(fh, sh) + (dot(fh, sl) + dot(fl, sh))


NARROW = [
    [index_of(2 * xh + xl, y, z, c) for y in range(4)[::-1] for xl in BITS[::-1]]
    for xh in BITS
    for z in range(4)
    for c in BITS
]


def gradient(pieces_ref):
    return jnp.concatenate([pieces_ref[7 - n] for n in range(8)], axis=0)


def thin_product(first, second, dims=((1,), (0,))):
    fh, fl = first
    sh, sl = second
    count = fh.shape[0]

    def dot(a, b):
        return lax.dot_general(a, b, (dims, ((), ())), preferred_element_type=jnp.float32)

    stacked = dot(jnp.concatenate([fh, fl], axis=0), sh)
    return stacked[:count] + (stacked[count:] + dot(fh, sl))


NT = ((1,), (1,))
TN = ((0,), (0,))


def pack_kernel(parts, table_ref, blocks, *rest):
    extra, outs = rest[: -len(parts)], rest[-len(parts) :]
    if extra:
        roots_kernel(*extra)
    here = [table_ref[16 + i] for i in range(3)]
    c = table_ref[19]
    targets = [c if own else 1 - c for own, _, _ in parts]
    cosets = [[coset_of(i, target, here[i]) for i in range(3)] for target in targets]

    def body(k, carry):
        for (_, half, streams), target, coset, out in zip(parts, targets, cosets, outs):
            offset = STREAM_TILES[streams[0]][0]
            for stream in streams:
                flips = [0, 0, 0]
                flips[stream] = half
                flips[(stream + 1) % 3] = (k >> 4) & 1
                flips[(stream + 2) % 3] = (k >> 3) & 1
                xd, yd, zd = (
                    member(i, target, coset[i] ^ flips[i], 1 - ((k >> (2 - i)) & 1)) for i in range(3)
                )
                block = table_ref[((xd >> 1) * 4 + zd) * 2 + target]
                row = (yd * 2 + (xd & 1)) * ROWS
                tiles = STREAM_TILES[stream]
                for pair in range(tiles[0] // 2, tiles[-1] // 2 + 1):
                    start = pl.multiple_of(row + (pair // 4) * 16, 16)
                    col = (pair % 4) * 128
                    value = blocks[0, block, pl.ds(start, 16), col : col + 128]
                    value = value.astype(jnp.float32)
                    for i in range(2):
                        if 2 * pair + i in tiles:
                            out[k, 2 * pair + i - offset] = value[8 * i : 8 * i + 8]
        return carry

    count = sum(len(streams) for _, _, streams in parts)
    lax.fori_loop(0, 32, body, 0, unroll=8 if count == 1 else 2)


def pack(name, parts, table, grads, matrices=()):
    extra = [jax.ShapeDtypeStruct((ORDER, ORDER), kind) for kind in ROOT_KINDS] if matrices else []
    packed = [
        jax.ShapeDtypeStruct((32, sum(len(STREAM_TILES[s]) for s in streams), 8, 128), jnp.float32)
        for _, _, streams in parts
    ]
    return pl.pallas_call(
        functools.partial(pack_kernel, parts),
        out_shape=extra + packed,
        in_specs=[pl.BlockSpec(memory_space=pltpu.SMEM)] + whole(1 + len(matrices)),
        out_specs=whole(len(extra) + len(parts)),
        compiler_params=pltpu.CompilerParams(vmem_limit_bytes=VMEM_LIMIT),
        name=name,
    )(table, grads, *matrices)


def cost(products, moved):
    return pl.CostEstimate(
        flops=6 * products * ORDER**3, bytes_accessed=moved, transcendentals=0
    )


HALF, FULL = jnp.bfloat16, jnp.float32
ROOT_KINDS = (FULL, HALF, HALF, FULL, HALF, HALF, HALF, HALF)


def roots_kernel(ls_ref, rs_ref, lr_ref, rr_ref, *outs):
    for stat_ref, root_ref, refs in ((ls_ref, lr_ref, outs[:3]), (rs_ref, rr_ref, outs[3:])):
        root = root_ref[0]
        parts = split(root)
        square = split(product(parts, parts))
        fourth = split(product(square, square))
        fifth = product(parts, fourth)
        base = 1.25 * root - (DECAY / 4.0) * product(split(fifth), split(stat_ref[0]))
        refs[0][...] = base
        refs[1][...], refs[2][...] = split(fifth * ((1.0 - DECAY) / 4.0))
        if len(refs) > 3:
            refs[3][...], refs[4][...] = split(base)


def whole(count):
    return [pl.BlockSpec(memory_space=pltpu.VMEM)] * count


def join_kernel(k0, r0, k1, r1, k2, r2, out):
    for tiles, kept, got in zip(STREAM_TILES, (k0, k1, k2), (r0, r1, r2)):
        out[:, tiles[0] : tiles[-1] + 1] = kept[...] + got[...]


def join(pieces):
    return pl.pallas_call(
        join_kernel,
        out_shape=jax.ShapeDtypeStruct((8, 32, 8, 128), jnp.float32),
        in_specs=whole(6),
        out_specs=pl.BlockSpec(memory_space=pltpu.VMEM),
        compiler_params=pltpu.CompilerParams(vmem_limit_bytes=SMALL_LIMIT),
        name="join",
    )(*pieces)


def total_kernel(parts, out):
    for tile in range(32):
        value = parts[0, tile]
        for i in range(1, 8):
            value = value + parts[i, tile]
        row, col = tile // 8 * 16 + tile % 2 * 8, tile // 2 % 4 * 128
        for i in range(8):
            out[i, row : row + 8, col : col + 128] = value


def total(parts):
    return pl.pallas_call(
        total_kernel,
        out_shape=jax.ShapeDtypeStruct((8, ROWS, ORDER), jnp.float32),
        in_specs=whole(1),
        out_specs=pl.BlockSpec(memory_space=pltpu.VMEM),
        compiler_params=pltpu.CompilerParams(vmem_limit_bytes=SMALL_LIMIT),
        name="total",
    )(parts)


def rows_kernel(table_ref, grad, lc, lkh, lkl, rkh, rkl, rch, rcl, out):
    g = split(gradient(grad))
    rows = pl.ds(pl.multiple_of(table_ref[20] * ROWS, ROWS), ROWS)
    inner = thin_product((lkh[rows, :], lkl[rows, :]), g)
    left = lc[rows, :] - thin_product(split(inner), g, NT)
    turned = split(thin_product(split(left), g))
    inner = thin_product(turned, (rkh[...], rkl[...]))
    inner = thin_product(split(inner), g, NT)
    value = thin_product(turned, (rch[...], rcl[...])) - thin_product(split(inner), g)
    for i in range(8):
        out[i] = value


def precondition_rows(table, grad, constants):
    return pl.pallas_call(
        rows_kernel,
        out_shape=jax.ShapeDtypeStruct((8, ROWS, ORDER), jnp.float32),
        in_specs=[pl.BlockSpec(memory_space=pltpu.SMEM)] + whole(8),
        out_specs=pl.BlockSpec(memory_space=pltpu.VMEM),
        compiler_params=pltpu.CompilerParams(vmem_limit_bytes=VMEM_LIMIT),
        name="rows",
    )(table, grad, *constants[:3], *constants[4:])


def stats_kernel(grad, lc, lkh, lkl, rc, rkh, rkl, ls, rs, ln, rn, li, ri):
    g = split(gradient(grad))
    for dims, stat_ref, c_ref, kh, kl, new_ref, inv_ref in (
        (NT, ls, lc, lkh, lkl, ln, li),
        (TN, rs, rc, rkh, rkl, rn, ri),
    ):
        gram = product(g, g, dims)
        new_ref[0] = DECAY * stat_ref[0] + (1.0 - DECAY) * gram
        inv_ref[0] = c_ref[...] - product((kh[...], kl[...]), split(gram))


def statistics(grad, constants, left_stat, right_stat):
    return pl.pallas_call(
        stats_kernel,
        out_shape=[jax.ShapeDtypeStruct((1, ORDER, ORDER), jnp.float32)] * 4,
        in_specs=whole(9),
        out_specs=whole(4),
        compiler_params=pltpu.CompilerParams(vmem_limit_bytes=VMEM_LIMIT),
        cost_estimate=cost(4, 11 << 20),
        name="stats",
    )(grad, *constants[:6], left_stat, right_stat)


def spread_kernel(late, table_ref, *refs):
    source, (out, sems) = refs[0], refs[-2:]
    core = 1 - table_ref[19] if late else table_ref[19]
    copies = [
        pltpu.make_async_copy(source.at[i], out.at[table_ref[2 * i + core]], sems.at[i])
        for i in range(8)
    ]
    for copy in copies:
        copy.start()
    for copy in copies:
        copy.wait()


def spread(table, source, before=None):
    late = before is not None
    anywhere = pl.BlockSpec(memory_space=pl.ANY)
    return pl.pallas_call(
        functools.partial(spread_kernel, late),
        out_shape=jax.ShapeDtypeStruct((16, ROWS, ORDER), jnp.float32),
        in_specs=[pl.BlockSpec(memory_space=pltpu.SMEM)] + whole(1) + [anywhere] * late,
        out_specs=anywhere,
        scratch_shapes=[pltpu.SemaphoreType.DMA((8,))],
        input_output_aliases={2: 0} if late else {},
        compiler_params=pltpu.CompilerParams(vmem_limit_bytes=SMALL_LIMIT),
        name="spread_late" if late else "spread",
    )(table, source, *([before] if late else []))


def local(replica_grads, owner_table, left_stat, right_stat, left_root, right_root):
    x, y, z, c = place()
    slots = jnp.arange(16, dtype=jnp.int32)
    block_of_slot = jnp.sum(
        jnp.where(owner_table[None, :] == slots[:, None], slots[None, :], 0), axis=1
    )
    coords = jnp.stack([x, y, z, c, y * 2 + (x & 1)]).astype(jnp.int32)
    table = jnp.concatenate([block_of_slot, coords])
    streams = range(3)
    everything = tuple(streams)
    arrived = []
    for s in streams:
        (value,) = pack(f"other{s}", [(False, 1, (s,))], table, replica_grads)
        table, value = lax.optimization_barrier((table, value))
        arrived.append(send(value, CORE_SWAP))
    mine = pack("own", [(True, 1, (s,)) for s in streams], table, replica_grads)
    table, mine = lax.optimization_barrier((table, mine))
    (other,) = pack("otherkeep", [(False, 0, everything)], table, replica_grads)
    outgoing = [mine[s] + arrived[s] for s in streams]
    table, other, _ = lax.optimization_barrier((table, other, outgoing))
    *constants, mine = pack(
        "keep",
        [(True, 0, everything)],
        table,
        replica_grads,
        (left_stat, right_stat, left_root, right_root),
    )
    arrived = send(other, CORE_SWAP)
    kept = [
        mine[:, tiles[0] : tiles[-1] + 1] + arrived[:, tiles[0] : tiles[-1] + 1]
        for tiles in STREAM_TILES
    ]
    tails = [None] * 3
    for step in range(3):
        for s in streams:
            axis = (s + step) % 3
            got = send(outgoing[s], axis_move(axis, first_masks(axis)))
            if step == 2:
                tails[s] = (kept[s], got)
                continue
            half = kept[s].shape[0] // 2
            outgoing[s] = kept[s][half:] + got[half:]
            kept[s] = kept[s][:half] + got[:half]
    joined = join([value for pair in tails for value in pair])
    parts = lax.all_to_all(joined, AXES, 0, 0, axis_index_groups=CUBES, tiled=True)
    grad = lax.all_to_all(total(parts), AXES, 0, 0, axis_index_groups=NARROW, tiled=True)
    rows = precondition_rows(table, grad, constants)
    got = lax.all_to_all(rows, ("xh", "z"), 0, 0, tiled=True)
    stats = statistics(grad, constants, left_stat, right_stat)
    got, stats = lax.optimization_barrier((got, stats))
    swapped = send(got, CORE_SWAP)
    directions = spread(table, swapped, spread(table, got))
    return (directions, *stats)


def solution(mesh):
    fine = Mesh(mesh.devices.reshape(SIZES), AXES)
    wide = ("xh", "z", "core")
    narrow = ("y", "xl")
    slot = P(wide, None, None)
    return jax.shard_map(
        local,
        mesh=fine,
        in_specs=(P(wide + narrow, None, None, None), P(), slot, slot, slot, slot),
        out_specs=(P(None, narrow, None), slot, slot, slot, slot),
        check_vma=False,
    )
```
